256 devices in a mesh: batch: 4 (over y), frame: 4 (over x_hi, core), space: 16 (over x_lo, z).
Axes of the slice: x: 4 (x_hi: 2, x_lo: 2; x = x_hi * 2 + x_lo), y: 4, z: 8, core: 2. Of those that a mesh axis runs over, the one named last changes fastest.
Arguments:
- queries: bfloat16 [32, 16, 8, 8, 1536], P(('batch', 'frame'), 'space'), parts along dimension 0, may hold values from -6 to 6
- keys: bfloat16 [32, 16, 8, 8, 1536], P(('batch', 'frame'), 'space'), parts along dimension 0, may hold values from -6 to 6
- values: bfloat16 [32, 16, 8, 8, 1536], P(('batch', 'frame'), 'space'), parts along dimension 0, may hold values from -6 to 6
- hidden: bfloat16 [32, 16, 8, 8, 3072], P(('batch', 'frame'), 'space'), parts along dimension 0, may hold values from -6 to 6
- control: bfloat16 [32, 16, 8, 8, 3072], P(('batch', 'frame'), 'space'), parts along dimension 0, may hold values from -4 to 4
- gate: bfloat16 [3072], replicated, may hold values from 0.5 to 3
- out_weight: bfloat16 [1536, 3072], P(('frame', 'space')), may hold values from -0.15625 to 0.15625
Outputs:
- output: bfloat16 [32, 16, 8, 8, 3072], P(('batch', 'frame'), 'space'), parts along dimension 0
The draws below stay inside these ranges and needn't reach their ends.
There are 4 independent parts, one for each index of `batch`. The reference program is written for one: setup_inputs(seed, part) draws one part's arguments, and reference() takes and returns one part's arrays. A program takes and returns all parts, laid end to end along the dimension named above; an argument that names none is the same for every part. Nothing has to cross between parts.
All inputs are finite; a program needn't handle non-finite values.
Results may differ from the reference program's by a relative error of at most 0.0034.
Values may be sent and summed in bfloat16 or wider, within the bound.
A program may use at most 128 MiB of HBM per device.

```python
import math
import jax
import jax.numpy as jnp
from jax import lax

D = 3072
HEADS = 12
HEAD_DIM = 128
TILE_F = 2
TILE_S = 8
HC = 1536
FRAMES = 8
BOXES = 16
GRID_W = 4
GRID_H = 4
N_FRAME = 4


def draw_queries(key, part):
    drawn = 1.4 * jax.random.normal(jax.random.fold_in(key, 1), (FRAMES * BOXES * TILE_S * TILE_S, HEADS, HEAD_DIM), jnp.float32)
    drawn = jnp.clip(drawn, -6.0, 6.0)
    return drawn.reshape(FRAMES, BOXES, TILE_S, TILE_S, HEADS * HEAD_DIM).astype(jnp.bfloat16)


def draw_keys(key, part):
    drawn = 1.4 * jax.random.normal(jax.random.fold_in(key, 2), (FRAMES * BOXES * TILE_S * TILE_S, HEADS, HEAD_DIM), jnp.float32)
    drawn = jnp.clip(drawn, -6.0, 6.0)
    return drawn.reshape(FRAMES, BOXES, TILE_S, TILE_S, HEADS * HEAD_DIM).astype(jnp.bfloat16)


def block_scale(key, dims, pieces, low, high):
    level, own = 1.0, jax.random.fold_in(key, 6)
    for dim, shards_of in pieces:
        steps = jnp.exp(jax.random.uniform(jax.random.fold_in(own, dim), (shards_of,), jnp.float32, low / len(pieces), high / len(pieces)))
        level = level * jnp.repeat(steps, dims[dim] // shards_of).reshape([-1 if axis == dim else 1 for axis in range(len(dims))])
    return level


def noise(stream_key, extent, scale, limit, shards=(), held_as=jnp.bfloat16):
    values = scale * jax.random.normal(stream_key, extent, jnp.float32)
    if shards:
        values = values * block_scale(stream_key, extent, shards, -0.22, 0.18)
    return jnp.clip(values, -limit, limit).astype(held_as)


def setup_inputs(seed: int = 0, part: int = 0) -> dict:
    key_list = jax.random.split(jax.random.key(seed), 8)
    part_keys = jax.random.split(jax.random.fold_in(key_list[7], part), 8)
    return {
        "queries": draw_queries(jax.random.fold_in(jax.random.fold_in(key_list[7], part), 71), part),
        "keys": draw_keys(jax.random.fold_in(jax.random.fold_in(key_list[7], part), 71), part),
        "values": noise(part_keys[2], (FRAMES, BOXES, TILE_S, TILE_S, HC), 1.0, 6.0, ((0, 4), (1, 16))),
        "hidden": noise(part_keys[3], (FRAMES, BOXES, TILE_S, TILE_S, D), 1.0, 6.0, ((0, 4), (1, 16))),
        "control": noise(part_keys[4], (FRAMES, BOXES, TILE_S, TILE_S, D), 0.5, 4.0, ((0, 4), (1, 16))),
        "gate": jnp.clip(jnp.exp(jax.random.uniform(key_list[5], (D,), jnp.float32, math.log(0.5), math.log(3.0))), 0.5, 3.0).astype(jnp.bfloat16),
        "out_weight": noise(key_list[6], (HC, D), HC ** -0.5, 0.15625, ((0, 64),)),
    }


def to_tiles(array):
    shaped = array.reshape(N_FRAME, TILE_F, GRID_H, GRID_W, TILE_S, TILE_S, HEADS, HEAD_DIM)
    shaped = shaped.transpose(0, 2, 3, 1, 4, 5, 6, 7)
    return shaped.reshape(N_FRAME, GRID_H, GRID_W, TILE_F * TILE_S * TILE_S, HEADS, HEAD_DIM)


def reference(queries, keys, values, hidden, control, gate, out_weight):
    per_tile = TILE_F * TILE_S * TILE_S
    score_scale = HEAD_DIM ** -0.5
    query_tiles = to_tiles(queries)
    padding = ((1, 1), (1, 1), (1, 1), (0, 0), (0, 0), (0, 0))
    key_tiles = jnp.pad(to_tiles(keys), padding)
    value_tiles = jnp.pad(to_tiles(values), padding)
    present = jnp.pad(jnp.ones((N_FRAME, GRID_H, GRID_W), jnp.float32), 1)

    def one_tile(tile_number):
        frame_pos = (tile_number // (GRID_H * GRID_W)).astype(jnp.int32)
        height_pos = (tile_number // GRID_W % GRID_H).astype(jnp.int32)
        width_pos = (tile_number % GRID_W).astype(jnp.int32)
        zero_pos = jnp.zeros((), jnp.int32)
        starts = (frame_pos, height_pos, width_pos, zero_pos, zero_pos, zero_pos)
        window_shape = (3, 3, 3, per_tile, HEADS, HEAD_DIM)
        window_keys = lax.dynamic_slice(key_tiles, starts, window_shape).reshape(27 * per_tile, HEADS, HEAD_DIM)
        window_values = lax.dynamic_slice(value_tiles, starts, window_shape).reshape(27 * per_tile, HEADS, HEAD_DIM)
        window_live = lax.dynamic_slice(present, starts[:3], (3, 3, 3)).reshape(27)
        live_keys = jnp.repeat(window_live, per_tile) > 0.5
        own_queries = lax.dynamic_slice(query_tiles, starts[:3] + (zero_pos, zero_pos, zero_pos),
                                        (1, 1, 1, per_tile, HEADS, HEAD_DIM)).reshape(per_tile, HEADS, HEAD_DIM)
        scores = jnp.einsum("qhe,khe->hqk", own_queries.astype(jnp.float32), window_keys.astype(jnp.float32)) * score_scale
        masked = jnp.where(live_keys[None, None, :], scores, -1e30)
        row_max = jnp.max(masked, axis=2, keepdims=True)
        weights = jnp.where(live_keys[None, None, :], jnp.exp(masked - row_max), 0.0)
        row_total = jnp.sum(weights, axis=2)
        rounded = weights.astype(jnp.bfloat16)
        blended = jnp.einsum("hqk,khe->qhe", rounded.astype(jnp.float32), window_values.astype(jnp.float32))
        return (blended / jnp.transpose(row_total)[:, :, None]).astype(jnp.bfloat16)

    tile_numbers = jnp.arange(N_FRAME * GRID_H * GRID_W, dtype=jnp.int32)
    outputs = lax.map(one_tile, tile_numbers)
    outputs = outputs.reshape(N_FRAME, GRID_H, GRID_W, TILE_F, TILE_S, TILE_S, HC)
    attention = outputs.transpose(0, 3, 1, 2, 4, 5, 6).reshape(-1, HC)
    projected = jnp.dot(attention, out_weight, preferred_element_type=jnp.float32)
    result = hidden.reshape(-1, D).astype(jnp.float32) + gate.astype(jnp.float32)[None, :] * projected
    result = result + control.reshape(-1, D).astype(jnp.float32)
    return result.astype(jnp.bfloat16).reshape(FRAMES, BOXES, TILE_S, TILE_S, D)
```

```python
import functools

import jax
import jax.numpy as jnp
from jax import lax
from jax.experimental import pallas as pl
from jax.experimental.pallas import tpu as pltpu
from jax.sharding import PartitionSpec as P

HD = 128
ROWS = 128
NH = 12
NB = 16
GW = 4
NY = 4
NF = 4
NZ = 8
MESH = pl.DeviceIdType.MESH
SCALE = HD ** -0.5 * 1.4426950408889634


def window(box):
    r, c = box // GW, box % GW
    return range(max(r - 1, 0), min(r + 2, GW)), max(c - 1, 0), min(c + 2, GW)


def kernel(q_hbm, k_hbm, v_hbm, w_hbm, attn, wfull,
           qbuf, kbuf, vbuf, obuf, mbuf, lbuf, acc,
           s_snd, k_rcv, v_rcv, q_rcv, h_snd, h_rcv, o_snd, o_rcv,
           w1s, w1r, w2s, w2r, w3s, w3r, w4s, w4r, w5s, w5r):
    y, f, s = lax.axis_index("batch"), lax.axis_index("frame"), lax.axis_index("space")
    lo, z = s // NZ, s % NZ
    hi, core = f // 2, f % 2
    quarter = wfull.shape[-1] // NY
    owner = s % 4 != 3
    my_head = (s // 4) * 3 + s % 4
    partner = f + 1 - 2 * core
    cross = f - 1 + 2 * core
    has_cross = (f == 1) | (f == 2)
    x = hi * 2 + lo
    xr, xl = (x + 1) % 4, (x + 3) % 4
    yr, yl = (y + 1) % NY, (y + NY - 1) % NY

    def at_x(pos):
        return (y, (pos // 2) * 2 + core, (pos % 2) * NZ + z)

    def wcols(yy):
        return pl.ds(pl.multiple_of(yy * quarter, 128), quarter)

    barrier = pltpu.get_barrier_semaphore()

    def greet(i, carry):
        pl.semaphore_signal(barrier, inc=1, device_id=(y, f, (s + i) % NB), device_id_type=MESH)
        return carry

    lax.fori_loop(1, NB, greet, 0)
    other_f = (f + 2) % NF
    for dev in ((y, other_f, s), (y, other_f, (s + NZ) % NB), (yr, f, s), (yl, f, s), (y, partner, s)):
        pl.semaphore_signal(barrier, inc=1, device_id=dev, device_id_type=MESH)

    @pl.when(has_cross)
    def _():
        pl.semaphore_signal(barrier, inc=1, device_id=(y, cross, s), device_id_type=MESH)

    pl.semaphore_wait(barrier, jnp.where(has_cross, NB + 5, NB + 4))

    def remote(src, dst, snd, rcv, dev):
        return pltpu.make_async_remote_copy(
            src_ref=src, dst_ref=dst, send_sem=snd, recv_sem=rcv, device_id=dev, device_id_type=MESH)

    def await_copy(ref, sem):
        pltpu.make_async_copy(ref, ref, sem).wait()

    def w1(i):
        zz = (z + i) % NZ
        return remote(w_hbm.at[:, wcols(y)], wfull.at[f, s, :, wcols(y)], w1s.at[zz], w1r.at[z],
                      (y, f, lo * NZ + zz))

    def start_w1(i, carry):
        w1(i).start()
        return carry

    pltpu.make_async_copy(w_hbm.at[:, wcols(y)], wfull.at[f, s, :, wcols(y)], w1r.at[z]).start()
    lax.fori_loop(1, NZ, start_w1, 0)

    first = (s // 4) * 3 + jnp.minimum(s % 4, 2)

    def head_of(i):
        h = (first + i) % NH
        return h, (h // 3) * 4 + h % 3

    def piece(ref, h):
        return ref.at[:, pl.ds(pl.multiple_of(h * HD, HD), HD)]

    streams = ((0, k_hbm, kbuf.at[0], k_rcv), (1, v_hbm, vbuf.at[0], v_rcv), (2, q_hbm, qbuf, q_rcv))

    def send_heads(which):
        def step(i, carry):
            h, to = head_of(i)
            for n in which:
                row, src, dst, rcv = streams[n]

                @pl.when(to == s)
                def _():
                    pltpu.make_async_copy(piece(src, h), dst.at[s], rcv.at[s]).start()

                @pl.when(to != s)
                def _():
                    remote(piece(src, h), dst.at[s], s_snd.at[row, h], rcv.at[s], (y, f, to)).start()
            return carry

        lax.fori_loop(0, NH, step, 0)

    send_heads((0, 1))
    send_heads((2,))

    def await_w1(i, carry):
        await_copy(wfull.at[f, lo * NZ + i, :, wcols(y)], w1r.at[i])
        return carry

    lax.fori_loop(0, NZ, await_w1, 0)

    def xblock(pos, start=0, count=NZ):
        return wfull.at[(pos // 2) * 2 + core, pl.ds((pos % 2) * NZ + start, count), :, wcols(y)]

    own_r = remote(xblock(x), xblock(x), w2s.at[0], w2r.at[0], at_x(xr))
    own_l = remote(xblock(x), xblock(x), w2s.at[1], w2r.at[1], at_x(xl))
    rel_r = remote(xblock(xl, 0, 4), xblock(xl, 0, 4), w2s.at[2], w2r.at[2], at_x(xr))
    rel_l = remote(xblock(xr, 4, 4), xblock(xr, 4, 4), w2s.at[3], w2r.at[3], at_x(xl))
    own_r.start()
    own_l.start()

    def forward(i):
        box = (s + NB - i) % NB
        out = []
        for n, (buf, rcv) in enumerate(((kbuf, k_rcv), (vbuf, v_rcv))):
            out.append((buf, rcv, box,
                        remote(buf.at[0, box], buf.at[1, box], h_snd.at[n, 0, box], h_rcv.at[n, 0, box],
                               (y, partner, s)),
                        remote(buf.at[0, box], buf.at[2, box], h_snd.at[n, 1, box], h_rcv.at[n, 1, box],
                               (y, cross, s))))
        return out

    def forward_step(i, carry):
        for buf, rcv, box, near, far in forward(i):
            await_copy(buf.at[0, box], rcv.at[box])

            @pl.when(has_cross)
            def _():
                far.start()

            near.start()
        return carry

    @pl.when(owner)
    def _():
        mbuf[...] = jnp.full_like(mbuf, -1e30)
        lbuf[...] = jnp.zeros_like(lbuf)
        acc[...] = jnp.zeros_like(acc)
        lax.fori_loop(0, 8, forward_step, 0)

    await_copy(xblock(xl), w2r.at[0])
    await_copy(xblock(xr), w2r.at[1])
    rel_r.start()
    rel_l.start()

    @pl.when(owner)
    def _():
        lax.fori_loop(8, NB, forward_step, 0)

    x2 = (x + 2) % 4
    await_copy(xblock(x2, 0, 4), w2r.at[2])
    await_copy(xblock(x2, 4, 4), w2r.at[3])

    def wblock(yy, n, side):
        return wfull.at[side + 2 * n, :, :, wcols(yy)]

    y2 = (y + 2) % NY

    def to_partner(n, m):
        yy = (y, yl, yr, y2)[n]
        return remote(wblock(yy, m, core), wblock(yy, m, core), w5s.at[2 * n + m], w5r.at[2 * n + m],
                      (y, partner, s))

    def y_own(d, m):
        return remote(wblock(y, m, core), wblock(y, m, core), w3s.at[2 * d + m], w3r.at[2 * d + m],
                      ((yr, yl)[d], f, s))

    y_rel = (remote(wblock(yl, 0, core), wblock(yl, 0, core), w4s.at[0], w4r.at[0], (yr, f, s)),
             remote(wblock(yr, 1, core), wblock(yr, 1, core), w4s.at[1], w4r.at[1], (yl, f, s)))
    for d, m in ((0, 0), (1, 1), (0, 1), (1, 0)):
        y_own(d, m).start()
    for m in (0, 1):
        to_partner(0, m).start()

    def relay_weight():
        await_copy(wblock(yl, 0, core), w3r.at[0])
        y_rel[0].start()
        await_copy(wblock(yr, 1, core), w3r.at[3])
        y_rel[1].start()
        to_partner(1, 0).start()
        to_partner(2, 1).start()
        await_copy(wblock(yl, 1, core), w3r.at[1])
        to_partner(1, 1).start()
        await_copy(wblock(yr, 0, core), w3r.at[2])
        to_partner(2, 0).start()

    frames = jnp.where(has_cross, 3, 2)

    def send_o(box, start):
        @pl.when(s == box)
        def _():
            if start:
                pltpu.make_async_copy(obuf.at[box], piece(attn, my_head), o_rcv.at[my_head]).start()

        @pl.when(s != box)
        def _():
            cp = remote(obuf.at[box], piece(attn, my_head), o_snd.at[box], o_rcv.at[my_head], (y, f, box))
            if start:
                cp.start()
            else:
                cp.wait_send()

    def one_frame(j, carry):
        @pl.when(j == 1)
        def _():
            relay_weight()

        for box in range(NB):
            rows, c0, c1 = window(box)
            if box % GW == 0:
                fresh = (0, 1) if box == 0 else ((box // GW + 1,) if box // GW + 1 < GW else ())

                @pl.when(j > 0)
                def _():
                    for r in fresh:
                        for b in range(r * GW, r * GW + GW):
                            await_copy(kbuf.at[j, b], h_rcv.at[0, j - 1, b])
                            await_copy(vbuf.at[j, b], h_rcv.at[1, j - 1, b])

            @pl.when(j == 0)
            def _():
                await_copy(qbuf.at[box], q_rcv.at[box])

            n = (c1 - c0) * ROWS
            q = qbuf[box]
            scores = [lax.dot_general(q, kbuf[j, r * GW + c0:r * GW + c1].reshape(n, HD),
                                      (((1,), (1,)), ((), ())), preferred_element_type=jnp.float32)
                      for r in rows]
            top = functools.reduce(jnp.maximum, scores)
            m_old = mbuf[box]
            m_new = jnp.maximum(m_old, jnp.max(top, axis=1, keepdims=True))
            alpha = jnp.exp2((m_old - m_new) * SCALE)
            shift = m_new[:, :1] * SCALE
            total = lbuf[box] * alpha
            out = acc[box] * alpha
            for r, sc in zip(rows, scores):
                p = jnp.exp2(sc * SCALE - shift)
                total = total + jnp.sum(p, axis=1, keepdims=True)
                out = out + jnp.dot(p.astype(jnp.bfloat16),
                                    vbuf[j, r * GW + c0:r * GW + c1].reshape(n, HD),
                                    preferred_element_type=jnp.float32)
            mbuf[box] = m_new
            lbuf[box] = total
            acc[box] = out

            @pl.when(j == frames - 1)
            def _():
                obuf[box] = (out / total).astype(jnp.bfloat16)
                if box:
                    send_o(box - 1, True)
        return carry

    @pl.when(owner)
    def _():
        lax.fori_loop(0, frames, one_frame, 0)
        send_o(NB - 1, True)

    @pl.when(jnp.logical_not(owner))
    def _():
        relay_weight()

    await_copy(wblock(y2, 0, core), w4r.at[0])
    to_partner(3, 0).start()
    await_copy(wblock(y2, 1, core), w4r.at[1])
    to_partner(3, 1).start()

    def await_o(h, carry):
        await_copy(piece(attn, h), o_rcv.at[h])
        return carry

    lax.fori_loop(0, NH, await_o, 0)
    for n in range(4):
        for m in (0, 1):
            await_copy(wblock((y, yl, yr, y2)[n], m, 1 - core), w5r.at[2 * n + m])

    def drain_heads(i, carry):
        h, to = head_of(i)

        @pl.when(to != s)
        def _():
            for row, src, dst, rcv in streams:
                remote(piece(src, h), dst.at[s], s_snd.at[row, h], rcv.at[s], (y, f, to)).wait_send()
        return carry

    lax.fori_loop(0, NH, drain_heads, 0)

    def drain_w1(i, carry):
        w1(i).wait_send()
        return carry

    lax.fori_loop(1, NZ, drain_w1, 0)
    for cp in (own_r, own_l, rel_r, rel_l) + y_rel:
        cp.wait_send()
    for d in (0, 1):
        for m in (0, 1):
            y_own(d, m).wait_send()
    for n in range(4):
        for m in (0, 1):
            to_partner(n, m).wait_send()

    @pl.when(owner)
    def _():
        def drain(i, carry):
            for _, _, _, near, far in forward(i):
                near.wait_send()

                @pl.when(has_cross)
                def _():
                    far.wait_send()
            return carry

        lax.fori_loop(0, NB, drain, 0)
        for box in range(NB):
            send_o(box, False)


def gather_and_attend(q, k, v, w):
    dma = pltpu.SemaphoreType.DMA
    any_spec = pl.BlockSpec(memory_space=pl.ANY)
    return pl.pallas_call(
        kernel,
        out_shape=(jax.ShapeDtypeStruct(q.shape, q.dtype),
                   jax.ShapeDtypeStruct((NF, NB) + w.shape, w.dtype)),
        in_specs=[any_spec] * 4,
        out_specs=(any_spec, any_spec),
        scratch_shapes=[
            pltpu.VMEM((NB, ROWS, HD), jnp.bfloat16),
            pltpu.VMEM((3, NB, ROWS, HD), jnp.bfloat16),
            pltpu.VMEM((3, NB, ROWS, HD), jnp.bfloat16),
            pltpu.VMEM((NB, ROWS, HD), jnp.bfloat16),
            pltpu.VMEM((NB, ROWS, HD), jnp.float32),
            pltpu.VMEM((NB, ROWS, HD), jnp.float32),
            pltpu.VMEM((NB, ROWS, HD), jnp.float32),
            dma((3, NH)), dma((NB,)), dma((NB,)), dma((NB,)),
            dma((2, 2, NB)), dma((2, 2, NB)), dma((NB,)), dma((NH,)),
            dma((NZ,)), dma((NZ,)), dma((4,)), dma((4,)), dma((4,)), dma((4,)),
            dma((2,)), dma((2,)), dma((8,)), dma((8,)),
        ],
        compiler_params=pltpu.CompilerParams(collective_id=0, has_side_effects=True,
                                             vmem_limit_bytes=48 * 1024 * 1024),
        name="gather_and_attend",
    )(q, k, v, w)


def per_device(queries, keys, values, hidden, control, gate, out_weight):
    channels = queries.shape[-1]
    width = out_weight.shape[1]
    flat = [a.reshape(-1, channels) for a in (queries, keys, values)]
    attention, weight = gather_and_attend(*flat, out_weight)
    projected = jnp.dot(attention, weight.reshape(channels, width), preferred_element_type=jnp.float32)
    result = hidden.reshape(-1, width).astype(jnp.float32) + gate.astype(jnp.float32)[None, :] * projected
    result = result + control.reshape(-1, width).astype(jnp.float32)
    return result.astype(jnp.bfloat16).reshape(hidden.shape)


def solution(mesh):
    tokens = P(("batch", "frame"), "space", None, None, None)
    return jax.shard_map(
        per_device,
        mesh=mesh,
        in_specs=(tokens,) * 5 + (P(), P(("frame", "space"), None)),
        out_specs=tokens,
        check_vma=False,
    )
```

```python
import functools

import jax
import jax.numpy as jnp
from jax import lax
from jax.experimental import pallas as pl
from jax.experimental.pallas import tpu as pltpu
from jax.sharding import PartitionSpec as P

HD = 128
ROWS = 128
NH = 12
NB = 16
GW = 4
NY = 4
NF = 4
NZ = 8
MESH = pl.DeviceIdType.MESH
SCALE = HD ** -0.5 * 1.4426950408889634


def kernel(q_hbm, k_hbm, v_hbm, w_hbm, attn, wfull,
           qbuf, kbuf, vbuf, vturn, obuf, sbuf, mbuf, abuf, lbuf, acc,
           s_snd, k_rcv, v_rcv, q_rcv, h_snd, h_rcv, o_snd, o_rcv,
           w1s, w1r, w2s, w2r, w3s, w3r, w4s, w4r, w5s, w5r):
    y, f, s = lax.axis_index("batch"), lax.axis_index("frame"), lax.axis_index("space")
    lo, z = s // NZ, s % NZ
    hi, core = f // 2, f % 2
    quarter = wfull.shape[-1] // NY
    owner = s % 4 != 3
    my_head = (s // 4) * 3 + s % 4
    partner = f + 1 - 2 * core
    cross = f - 1 + 2 * core
    has_cross = (f == 1) | (f == 2)
    x = hi * 2 + lo
    xr, xl = (x + 1) % 4, (x + 3) % 4
    yr, yl = (y + 1) % NY, (y + NY - 1) % NY

    def at_x(pos):
        return (y, (pos // 2) * 2 + core, (pos % 2) * NZ + z)

    def wcols(yy):
        return pl.ds(pl.multiple_of(yy * quarter, 128), quarter)

    barrier = pltpu.get_barrier_semaphore()

    def greet(i, carry):
        pl.semaphore_signal(barrier, inc=1, device_id=(y, f, (s + i) % NB), device_id_type=MESH)
        return carry

    lax.fori_loop(1, NB, greet, 0)
    other_f = (f + 2) % NF
    for dev in ((y, other_f, s), (y, other_f, (s + NZ) % NB), (yr, f, s), (yl, f, s), (y, partner, s)):
        pl.semaphore_signal(barrier, inc=1, device_id=dev, device_id_type=MESH)

    @pl.when(has_cross)
    def _():
        pl.semaphore_signal(barrier, inc=1, device_id=(y, cross, s), device_id_type=MESH)

    pl.semaphore_wait(barrier, jnp.where(has_cross, NB + 5, NB + 4))

    def remote(src, dst, snd, rcv, dev):
        return pltpu.make_async_remote_copy(
            src_ref=src, dst_ref=dst, send_sem=snd, recv_sem=rcv, device_id=dev, device_id_type=MESH)

    def await_copy(ref, sem):
        pltpu.make_async_copy(ref, ref, sem).wait()

    def w1(i):
        zz = (z + i) % NZ
        return remote(w_hbm.at[:, wcols(y)], wfull.at[f, s, :, wcols(y)], w1s.at[zz], w1r.at[z],
                      (y, f, lo * NZ + zz))

    def start_w1(i, carry):
        w1(i).start()
        return carry

    pltpu.make_async_copy(w_hbm.at[:, wcols(y)], wfull.at[f, s, :, wcols(y)], w1r.at[z]).start()
    lax.fori_loop(1, NZ, start_w1, 0)

    first = (s // 4) * 3 + jnp.minimum(s % 4, 2)

    def head_of(i):
        h = (first + i) % NH
        return h, (h // 3) * 4 + h % 3

    def piece(ref, h):
        return ref.at[:, pl.ds(pl.multiple_of(h * HD, HD), HD)]

    streams = ((0, k_hbm, kbuf.at[0], k_rcv), (1, v_hbm, vbuf.at[0], v_rcv), (2, q_hbm, qbuf, q_rcv))

    def send_heads(which):
        def step(i, carry):
            h, to = head_of(i)
            for n in which:
                row, src, dst, rcv = streams[n]

                @pl.when(to == s)
                def _():
                    pltpu.make_async_copy(piece(src, h), dst.at[s], rcv.at[s]).start()

                @pl.when(to != s)
                def _():
                    remote(piece(src, h), dst.at[s], s_snd.at[row, h], rcv.at[s], (y, f, to)).start()
            return carry

        lax.fori_loop(0, NH, step, 0)

    send_heads((0, 1))
    send_heads((2,))

    def await_w1(i, carry):
        await_copy(wfull.at[f, lo * NZ + i, :, wcols(y)], w1r.at[i])
        return carry

    lax.fori_loop(0, NZ, await_w1, 0)

    def xblock(pos, start=0, count=NZ):
        return wfull.at[(pos // 2) * 2 + core, pl.ds((pos % 2) * NZ + start, count), :, wcols(y)]

    own_r = remote(xblock(x), xblock(x), w2s.at[0], w2r.at[0], at_x(xr))
    own_l = remote(xblock(x), xblock(x), w2s.at[1], w2r.at[1], at_x(xl))
    rel_r = remote(xblock(xl, 0, 4), xblock(xl, 0, 4), w2s.at[2], w2r.at[2], at_x(xr))
    rel_l = remote(xblock(xr, 4, 4), xblock(xr, 4, 4), w2s.at[3], w2r.at[3], at_x(xl))
    own_r.start()
    own_l.start()

    def forward(i):
        box = (s + NB - i) % NB
        out = []
        for n, (buf, rcv) in enumerate(((kbuf, k_rcv), (vbuf, v_rcv))):
            out.append((buf, rcv, box,
                        remote(buf.at[0, box], buf.at[1, box], h_snd.at[n, 0, box], h_rcv.at[n, 0, box],
                               (y, partner, s)),
                        remote(buf.at[0, box], buf.at[2, box], h_snd.at[n, 1, box], h_rcv.at[n, 1, box],
                               (y, cross, s))))
        return out

    def forward_step(i, carry):
        for buf, rcv, box, near, far in forward(i):
            await_copy(buf.at[0, box], rcv.at[box])

            @pl.when(has_cross)
            def _():
                far.start()

            near.start()
        return carry

    @pl.when(owner)
    def _():
        mbuf[...] = jnp.full_like(mbuf, -1e30)
        lbuf[...] = jnp.zeros_like(lbuf)
        acc[...] = jnp.zeros_like(acc)
        lax.fori_loop(0, 8, forward_step, 0)

    await_copy(xblock(xl), w2r.at[0])
    await_copy(xblock(xr), w2r.at[1])
    rel_r.start()
    rel_l.start()

    @pl.when(owner)
    def _():
        lax.fori_loop(8, NB, forward_step, 0)

    x2 = (x + 2) % 4
    await_copy(xblock(x2, 0, 4), w2r.at[2])
    await_copy(xblock(x2, 4, 4), w2r.at[3])

    def wblock(yy, n, side):
        return wfull.at[side + 2 * n, :, :, wcols(yy)]

    y2 = (y + 2) % NY

    def to_partner(n, m):
        yy = (y, yl, yr, y2)[n]
        return remote(wblock(yy, m, core), wblock(yy, m, core), w5s.at[2 * n + m], w5r.at[2 * n + m],
                      (y, partner, s))

    def y_own(d, m):
        return remote(wblock(y, m, core), wblock(y, m, core), w3s.at[2 * d + m], w3r.at[2 * d + m],
                      ((yr, yl)[d], f, s))

    y_rel = (remote(wblock(yl, 0, core), wblock(yl, 0, core), w4s.at[0], w4r.at[0], (yr, f, s)),
             remote(wblock(yr, 1, core), wblock(yr, 1, core), w4s.at[1], w4r.at[1], (yl, f, s)))
    for d, m in ((0, 0), (1, 1), (0, 1), (1, 0)):
        y_own(d, m).start()
    for m in (0, 1):
        to_partner(0, m).start()

    def relay_weight():
        await_copy(wblock(yl, 0, core), w3r.at[0])
        y_rel[0].start()
        await_copy(wblock(yr, 1, core), w3r.at[3])
        y_rel[1].start()
        to_partner(1, 0).start()
        to_partner(2, 1).start()
        await_copy(wblock(yl, 1, core), w3r.at[1])
        to_partner(1, 1).start()
        await_copy(wblock(yr, 0, core), w3r.at[2])
        to_partner(2, 0).start()

    frames = jnp.where(has_cross, 3, 2)

    def send_o(box, start):
        @pl.when(s == box)
        def _():
            if start:
                pltpu.make_async_copy(obuf.at[box], piece(attn, my_head), o_rcv.at[my_head]).start()

        @pl.when(s != box)
        def _():
            cp = remote(obuf.at[box], piece(attn, my_head), o_snd.at[box], o_rcv.at[my_head], (y, f, box))
            if start:
                cp.start()
            else:
                cp.wait_send()

    spans = ((0, 2), (0, 3), (0, 3), (1, 3))

    def around(k):
        r = k // 2
        return r, k % 2, range(max(r - 1, 0), min(r + 2, GW))

    def score(j, k):
        r, pair, rows = around(k)
        box = r * GW + 2 * pair
        q = qbuf[box:box + 2].reshape(2 * ROWS, HD)
        tops = [[], []]
        for i, g in enumerate(rows):
            sc = lax.dot_general(kbuf[j, g * GW + pair:g * GW + pair + 3].reshape(3 * ROWS, HD), q,
                                 (((1,), (1,)), ((), ())), preferred_element_type=jnp.float32)
            sbuf[k % 2, i * 3 * ROWS:(i + 1) * 3 * ROWS] = sc
            for side in (0, 1):
                k0, k1 = spans[2 * pair + side]
                tops[side].append(jnp.max(sc[k0 * ROWS:k1 * ROWS, side * ROWS:side * ROWS + ROWS],
                                          axis=0, keepdims=True))
        for side in (0, 1):
            m_old = mbuf[box + side]
            m_new = functools.reduce(jnp.maximum, tops[side], m_old)
            mbuf[box + side] = m_new
            abuf[box + side] = jnp.exp2((m_old - m_new) * SCALE)

    def blend(k):
        r, pair, rows = around(k)
        for side in (0, 1):
            box = r * GW + 2 * pair + side
            k0, k1 = spans[2 * pair + side]
            shift = mbuf[box] * SCALE
            total = lbuf[box] * abuf[box]
            out = acc[box] * abuf[box]
            for i, g in enumerate(rows):
                sc = sbuf[k % 2, (3 * i + k0) * ROWS:(3 * i + k1) * ROWS, side * ROWS:side * ROWS + ROWS]
                p = jnp.exp2(sc * SCALE - shift)
                total = total + jnp.sum(p, axis=0, keepdims=True)
                c = (g * GW + pair + k0) * ROWS
                out = out + jnp.dot(vturn[:, c:c + (k1 - k0) * ROWS], p.astype(jnp.bfloat16),
                                    preferred_element_type=jnp.float32)
            lbuf[box] = total
            acc[box] = out

    def finish(r):
        for box in range(r * GW, r * GW + GW):
            obuf[box] = (acc[box] / lbuf[box]).T.astype(jnp.bfloat16)
        for box in range(r * GW - GW, r * GW):
            if box >= 0:
                send_o(box, True)

    def one_frame(j, carry):
        @pl.when(j == 1)
        def _():
            relay_weight()

        for r in range(GW):
            fresh = range(0, 2) if r == 0 else range(r + 1, min(r + 2, GW))

            @pl.when(j > 0)
            def _():
                for b in (g * GW + c for g in fresh for c in range(GW)):
                    await_copy(kbuf.at[j, b], h_rcv.at[0, j - 1, b])
                    await_copy(vbuf.at[j, b], h_rcv.at[1, j - 1, b])

            @pl.when(j == 0)
            def _():
                for box in range(r * GW, r * GW + GW):
                    await_copy(qbuf.at[box], q_rcv.at[box])

            for b in (g * GW + c for g in fresh for c in range(GW)):
                vturn[:, b * ROWS:b * ROWS + ROWS] = vbuf[j, b].T
            score(j, 2 * r)
            if r:
                blend(2 * r - 1)

                @pl.when(j == frames - 1)
                def _():
                    finish(r - 1)
            score(j, 2 * r + 1)
            blend(2 * r)

        blend(2 * GW - 1)

        @pl.when(j == frames - 1)
        def _():
            finish(GW - 1)
        return carry

    @pl.when(owner)
    def _():
        lax.fori_loop(0, frames, one_frame, 0)
        for box in range(NB - GW, NB):
            send_o(box, True)

    @pl.when(jnp.logical_not(owner))
    def _():
        relay_weight()

    await_copy(wblock(y2, 0, core), w4r.at[0])
    to_partner(3, 0).start()
    await_copy(wblock(y2, 1, core), w4r.at[1])
    to_partner(3, 1).start()

    def await_o(h, carry):
        await_copy(piece(attn, h), o_rcv.at[h])
        return carry

    lax.fori_loop(0, NH, await_o, 0)
    for n in range(4):
        for m in (0, 1):
            await_copy(wblock((y, yl, yr, y2)[n], m, 1 - core), w5r.at[2 * n + m])

    def drain_heads(i, carry):
        h, to = head_of(i)

        @pl.when(to != s)
        def _():
            for row, src, dst, rcv in streams:
                remote(piece(src, h), dst.at[s], s_snd.at[row, h], rcv.at[s], (y, f, to)).wait_send()
        return carry

    lax.fori_loop(0, NH, drain_heads, 0)

    def drain_w1(i, carry):
        w1(i).wait_send()
        return carry

    lax.fori_loop(1, NZ, drain_w1, 0)
    for cp in (own_r, own_l, rel_r, rel_l) + y_rel:
        cp.wait_send()
    for d in (0, 1):
        for m in (0, 1):
            y_own(d, m).wait_send()
    for n in range(4):
        for m in (0, 1):
            to_partner(n, m).wait_send()

    @pl.when(owner)
    def _():
        def drain(i, carry):
            for _, _, _, near, far in forward(i):
                near.wait_send()

                @pl.when(has_cross)
                def _():
                    far.wait_send()
            return carry

        lax.fori_loop(0, NB, drain, 0)
        for box in range(NB):
            send_o(box, False)


def gather_and_attend(q, k, v, w):
    dma = pltpu.SemaphoreType.DMA
    any_spec = pl.BlockSpec(memory_space=pl.ANY)
    return pl.pallas_call(
        kernel,
        out_shape=(jax.ShapeDtypeStruct(q.shape, q.dtype),
                   jax.ShapeDtypeStruct((NF, NB) + w.shape, w.dtype)),
        in_specs=[any_spec] * 4,
        out_specs=(any_spec, any_spec),
        scratch_shapes=[
            pltpu.VMEM((NB, ROWS, HD), jnp.bfloat16),
            pltpu.VMEM((3, NB, ROWS, HD), jnp.bfloat16),
            pltpu.VMEM((3, NB, ROWS, HD), jnp.bfloat16),
            pltpu.VMEM((HD, NB * ROWS), jnp.bfloat16),
            pltpu.VMEM((NB, ROWS, HD), jnp.bfloat16),
            pltpu.VMEM((2, 9 * ROWS, 2 * ROWS), jnp.float32),
            pltpu.VMEM((NB, 1, ROWS), jnp.float32),
            pltpu.VMEM((NB, 1, ROWS), jnp.float32),
            pltpu.VMEM((NB, 1, ROWS), jnp.float32),
            pltpu.VMEM((NB, HD, ROWS), jnp.float32),
            dma((3, NH)), dma((NB,)), dma((NB,)), dma((NB,)),
            dma((2, 2, NB)), dma((2, 2, NB)), dma((NB,)), dma((NH,)),
            dma((NZ,)), dma((NZ,)), dma((4,)), dma((4,)), dma((4,)), dma((4,)),
            dma((2,)), dma((2,)), dma((8,)), dma((8,)),
        ],
        compiler_params=pltpu.CompilerParams(collective_id=0, has_side_effects=True,
                                             vmem_limit_bytes=62 * 1024 * 1024),
        name="gather_and_attend",
    )(q, k, v, w)


def per_device(queries, keys, values, hidden, control, gate, out_weight):
    channels = queries.shape[-1]
    width = out_weight.shape[1]
    flat = [a.reshape(-1, channels) for a in (queries, keys, values)]
    attention, weight = gather_and_attend(*flat, out_weight)
    projected = jnp.dot(attention, weight.reshape(channels, width), preferred_element_type=jnp.float32)
    result = hidden.reshape(-1, width).astype(jnp.float32) + gate.astype(jnp.float32)[None, :] * projected
    result = result + control.reshape(-1, width).astype(jnp.float32)
    return result.astype(jnp.bfloat16).reshape(hidden.shape)


def solution(mesh):
    tokens = P(("batch", "frame"), "space", None, None, None)
    return jax.shard_map(
        per_device,
        mesh=mesh,
        in_specs=(tokens,) * 5 + (P(), P(("frame", "space"), None)),
        out_specs=tokens,
        check_vma=False,
    )
```

```python
import functools

import jax
import jax.numpy as jnp
from jax import lax
from jax.experimental import pallas as pl
from jax.experimental.pallas import tpu as pltpu
from jax.sharding import PartitionSpec as P

HD = 128
ROWS = 128
NH = 12
NB = 16
GW = 4
NY = 4
NF = 4
NZ = 8
MESH = pl.DeviceIdType.MESH
SCALE = HD ** -0.5 * 1.4426950408889634


def kernel(q_hbm, k_hbm, v_hbm, w_hbm, attn, wfull,
           qbuf, kbuf, vbuf, vturn, obuf, sbuf, mbuf, abuf, lbuf, acc,
           s_snd, k_rcv, v_rcv, q_rcv, h_snd, h_rcv, o_snd, o_rcv,
           w1s, w1r, w2s, w2r, w3s, w3r, w4s, w4r, w5s, w5r):
    y, f, s = lax.axis_index("batch"), lax.axis_index("frame"), lax.axis_index("space")
    lo, z = s // NZ, s % NZ
    hi, core = f // 2, f % 2
    quarter = wfull.shape[-1] // NY
    owner = jnp.where(s < NZ, s % 4 != 3, s % 4 != 1)
    my_head = (s // 4) * 3 + s % 4 - jnp.where((s >= NZ) & (s % 4 > 1), 1, 0)
    partner = f + 1 - 2 * core
    cross = f - 1 + 2 * core
    has_cross = (f == 1) | (f == 2)
    x = hi * 2 + lo
    xr, xl = (x + 1) % 4, (x + 3) % 4
    yr, yl = (y + 1) % NY, (y + NY - 1) % NY

    def at_x(pos):
        return (y, (pos // 2) * 2 + core, (pos % 2) * NZ + z)

    def wcols(yy):
        return pl.ds(pl.multiple_of(yy * quarter, 128), quarter)

    barrier = pltpu.get_barrier_semaphore()

    def greet(i, carry):
        pl.semaphore_signal(barrier, inc=1, device_id=(y, f, (s + i) % NB), device_id_type=MESH)
        return carry

    lax.fori_loop(1, NB, greet, 0)
    other_f = (f + 2) % NF
    for dev in ((y, other_f, s), (y, other_f, (s + NZ) % NB), (yr, f, s), (yl, f, s), (y, partner, s)):
        pl.semaphore_signal(barrier, inc=1, device_id=dev, device_id_type=MESH)

    @pl.when(has_cross)
    def _():
        pl.semaphore_signal(barrier, inc=1, device_id=(y, cross, s), device_id_type=MESH)

    pl.semaphore_wait(barrier, jnp.where(has_cross, NB + 5, NB + 4))

    def remote(src, dst, snd, rcv, dev):
        return pltpu.make_async_remote_copy(
            src_ref=src, dst_ref=dst, send_sem=snd, recv_sem=rcv, device_id=dev, device_id_type=MESH)

    def await_copy(ref, sem):
        pltpu.make_async_copy(ref, ref, sem).wait()

    def w1(i):
        zz = (z + i) % NZ
        return remote(w_hbm.at[:, wcols(y)], wfull.at[f, s, :, wcols(y)], w1s.at[zz], w1r.at[z],
                      (y, f, lo * NZ + zz))

    def start_w1(i, carry):
        w1(i).start()
        return carry

    pltpu.make_async_copy(w_hbm.at[:, wcols(y)], wfull.at[f, s, :, wcols(y)], w1r.at[z]).start()
    lax.fori_loop(1, NZ, start_w1, 0)

    first = jnp.minimum(my_head, NH - 1)

    def head_of(i):
        h = (first + i) % NH
        return h, (h // 3) * 4 + h % 3 + jnp.where((h >= NH // 2) & (h % 3 > 0), 1, 0)

    def piece(ref, h):
        return ref.at[:, pl.ds(pl.multiple_of(h * HD, HD), HD)]

    streams = ((0, k_hbm, kbuf.at[0], k_rcv), (1, v_hbm, vbuf.at[0], v_rcv), (2, q_hbm, qbuf, q_rcv))

    def send_heads(which):
        def step(i, carry):
            h, to = head_of(i)
            for n in which:
                row, src, dst, rcv = streams[n]

                @pl.when(to == s)
                def _():
                    pltpu.make_async_copy(piece(src, h), dst.at[s], rcv.at[s]).start()

                @pl.when(to != s)
                def _():
                    remote(piece(src, h), dst.at[s], s_snd.at[row, h], rcv.at[s], (y, f, to)).start()
            return carry

        lax.fori_loop(0, NH, step, 0)

    send_heads((0, 1))
    send_heads((2,))

    places = (x, xl, xr, (x + 2) % 4)
    layers = (y, yl, yr, (y + 2) % NY)
    halves = ((0, NZ // 2), (NZ // 2, NZ // 2))

    def block(n, m=0, side=core, part=(0, NZ)):
        pos = places[n]
        return wfull.at[(pos // 2) * 2 + side, pl.ds((pos % 2) * NZ + part[0], part[1]), :, wcols(layers[m])]

    def push(ref, snd, rcv, dev):
        return remote(ref, ref, snd, rcv, dev)

    x_own = (push(block(0), w2s.at[0], w2r.at[0], at_x(xr)), push(block(0), w2s.at[1], w2r.at[1], at_x(xl)))
    x_rel = (push(block(1, part=halves[0]), w2s.at[2], w2r.at[2], at_x(xr)),
             push(block(2, part=halves[1]), w2s.at[3], w2r.at[3], at_x(xl)))

    def y_own(d, n):
        return push(block(n), w3s.at[4 * d + n], w3r.at[4 * d + n], ((yr, yl)[d], f, s))

    def y_rel(n):
        return push(block(n, 1), w4s.at[n], w4r.at[n], (yr, f, s)) if n < 2 else \
            push(block(n, 2), w4s.at[n], w4r.at[n], (yl, f, s))

    def to_partner(m, n):
        return push(block(n, m), w5s.at[4 * m + n], w5r.at[4 * m + n], (y, partner, s))

    def spread(n):
        y_own(0, n).start()
        y_own(1, n).start()
        to_partner(0, n).start()

    def weight_z():
        lax.fori_loop(0, NZ, await_w1, 0)
        x_own[0].start()
        x_own[1].start()
        spread(0)

    def weight_x():
        await_copy(block(1), w2r.at[0])
        x_rel[0].start()
        spread(1)
        await_copy(block(2), w2r.at[1])
        x_rel[1].start()
        spread(2)

    def weight_x2():
        await_copy(block(3, part=halves[0]), w2r.at[2])
        await_copy(block(3, part=halves[1]), w2r.at[3])
        spread(3)

    def weight_y(n):
        await_copy(block(n, 1), w3r.at[n])
        if n < 2:
            y_rel(n).start()
        to_partner(1, n).start()
        await_copy(block(n, 2), w3r.at[4 + n])
        if n >= 2:
            y_rel(n).start()
        to_partner(2, n).start()

    def weight_y2(n):
        await_copy(block(n, 3), w4r.at[n])
        to_partner(3, n).start()

    def await_w1(i, carry):
        await_copy(wfull.at[f, lo * NZ + i, :, wcols(y)], w1r.at[i])
        return carry

    def forward(i):
        box = (s + NB - i) % NB
        out = []
        for n, (buf, rcv) in enumerate(((kbuf, k_rcv), (vbuf, v_rcv))):
            out.append((buf, rcv, box,
                        remote(buf.at[0, box], buf.at[1, box], h_snd.at[n, 0, box], h_rcv.at[n, 0, box],
                               (y, partner, s)),
                        remote(buf.at[0, box], buf.at[2, box], h_snd.at[n, 1, box], h_rcv.at[n, 1, box],
                               (y, cross, s))))
        return out

    def forward_step(i, carry):
        for buf, rcv, box, near, far in forward(i):
            await_copy(buf.at[0, box], rcv.at[box])

            @pl.when(has_cross)
            def _():
                far.start()

            near.start()
        return carry

    weight_steps = (weight_z, weight_x, weight_x2) + tuple(functools.partial(weight_y, n) for n in range(4))

    @pl.when(owner)
    def _():
        mbuf[...] = jnp.full_like(mbuf, -1e30)
        lbuf[...] = jnp.zeros_like(lbuf)
        acc[...] = jnp.zeros_like(acc)
        marks = (0, 2, 4, 6, 8, 11, 14, NB)
        for step, i0, i1 in zip(weight_steps, marks, marks[1:]):
            step()
            lax.fori_loop(i0, i1, forward_step, 0)

    @pl.when(jnp.logical_not(owner))
    def _():
        for step in weight_steps:
            step()
        for n in range(4):
            weight_y2(n)

    frames = jnp.where(has_cross, 3, 2)

    def send_o(box, start):
        @pl.when(s == box)
        def _():
            if start:
                pltpu.make_async_copy(obuf.at[box], piece(attn, my_head), o_rcv.at[my_head]).start()

        @pl.when(s != box)
        def _():
            cp = remote(obuf.at[box], piece(attn, my_head), o_snd.at[box], o_rcv.at[my_head], (y, f, box))
            if start:
                cp.start()
            else:
                cp.wait_send()

    spans = ((0, 2), (0, 3), (0, 3), (1, 3))

    def around(k):
        r = k // 2
        return r, k % 2, range(max(r - 1, 0), min(r + 2, GW))

    def score(j, k):
        r, pair, rows = around(k)
        box = r * GW + 2 * pair
        q = qbuf[box:box + 2].reshape(2 * ROWS, HD)
        tops = [[], []]
        for i, g in enumerate(rows):
            sc = lax.dot_general(kbuf[j, g * GW + pair:g * GW + pair + 3].reshape(3 * ROWS, HD), q,
                                 (((1,), (1,)), ((), ())), preferred_element_type=jnp.float32)
            sbuf[k % 2, i * 3 * ROWS:(i + 1) * 3 * ROWS] = sc
            for side in (0, 1):
                k0, k1 = spans[2 * pair + side]
                tops[side].append(jnp.max(sc[k0 * ROWS:k1 * ROWS, side * ROWS:side * ROWS + ROWS],
                                          axis=0, keepdims=True))
        for side in (0, 1):
            m_old = mbuf[box + side]
            m_new = functools.reduce(jnp.maximum, tops[side], m_old)
            mbuf[box + side] = m_new
            abuf[box + side] = jnp.exp2((m_old - m_new) * SCALE)

    def blend(j, k):
        r, pair, rows = around(k)
        for side in (0, 1):
            box = r * GW + 2 * pair + side
            k0, k1 = spans[2 * pair + side]
            shift = mbuf[box] * SCALE
            total = lbuf[box] * abuf[box]
            out = acc[box] * abuf[box]
            for i, g in enumerate(rows):
                sc = sbuf[k % 2, (3 * i + k0) * ROWS:(3 * i + k1) * ROWS, side * ROWS:side * ROWS + ROWS]
                p = jnp.exp2(sc * SCALE - shift)
                total = total + jnp.sum(p, axis=0, keepdims=True)
                c = (g * GW + pair + k0) * ROWS
                out = out + jnp.dot(vturn[j, :, c:c + (k1 - k0) * ROWS], p.astype(jnp.bfloat16),
                                    preferred_element_type=jnp.float32)
            lbuf[box] = total
            acc[box] = out

    def finish(r):
        for box in range(r * GW, r * GW + GW):
            obuf[box] = (acc[box] / lbuf[box]).T.astype(jnp.bfloat16)

    def send_row(r):
        for box in range(r * GW, r * GW + GW):
            send_o(box, True)

    def attend_row(r):
        fresh = [g * GW + c for g in (range(0, 2) if r == 0 else range(r + 1, min(r + 2, GW))) for c in range(GW)]

        def await_halo(j):
            for b in fresh:
                await_copy(kbuf.at[j, b], h_rcv.at[0, j - 1, b])
                await_copy(vbuf.at[j, b], h_rcv.at[1, j - 1, b])

        await_halo(1)

        @pl.when(has_cross)
        def _():
            await_halo(2)

        for box in range(r * GW, r * GW + GW):
            await_copy(qbuf.at[box], q_rcv.at[box])
        score(0, 2 * r)
        if r:
            send_row(r - 1)

        def one_frame(j, carry):
            for b in fresh:
                vturn[j, :, b * ROWS:b * ROWS + ROWS] = vbuf[j, b].T
            score(j, 2 * r + 1)
            blend(j, 2 * r)
            score(jnp.minimum(j + 1, frames - 1), 2 * r)
            blend(j, 2 * r + 1)
            return carry

        lax.fori_loop(0, frames, one_frame, 0)
        finish(r)

    @pl.when(owner)
    def _():
        for r in range(GW):
            attend_row(r)
            if r >= 2:
                weight_y2(2 * r - 4)
                weight_y2(2 * r - 3)
        send_row(GW - 1)

    def await_o(h, carry):
        await_copy(piece(attn, h), o_rcv.at[h])
        return carry

    lax.fori_loop(0, NH, await_o, 0)
    for m in range(4):
        for n in range(4):
            await_copy(block(n, m, 1 - core), w5r.at[4 * m + n])

    def drain_heads(i, carry):
        h, to = head_of(i)

        @pl.when(to != s)
        def _():
            for row, src, dst, rcv in streams:
                remote(piece(src, h), dst.at[s], s_snd.at[row, h], rcv.at[s], (y, f, to)).wait_send()
        return carry

    lax.fori_loop(0, NH, drain_heads, 0)

    def drain_w1(i, carry):
        w1(i).wait_send()
        return carry

    lax.fori_loop(1, NZ, drain_w1, 0)
    for cp in x_own + x_rel:
        cp.wait_send()
    for n in range(4):
        y_own(0, n).wait_send()
        y_own(1, n).wait_send()
        y_rel(n).wait_send()
        for m in range(4):
            to_partner(m, n).wait_send()

    @pl.when(owner)
    def _():
        def drain(i, carry):
            for _, _, _, near, far in forward(i):
                near.wait_send()

                @pl.when(has_cross)
                def _():
                    far.wait_send()
            return carry

        lax.fori_loop(0, NB, drain, 0)
        for box in range(NB):
            send_o(box, False)


def gather_and_attend(q, k, v, w):
    dma = pltpu.SemaphoreType.DMA
    any_spec = pl.BlockSpec(memory_space=pl.ANY)
    return pl.pallas_call(
        kernel,
        out_shape=(jax.ShapeDtypeStruct(q.shape, q.dtype),
                   jax.ShapeDtypeStruct((NF, NB) + w.shape, w.dtype)),
        in_specs=[any_spec] * 4,
        out_specs=(any_spec, any_spec),
        scratch_shapes=[
            pltpu.VMEM((NB, ROWS, HD), jnp.bfloat16),
            pltpu.VMEM((3, NB, ROWS, HD), jnp.bfloat16),
            pltpu.VMEM((3, NB, ROWS, HD), jnp.bfloat16),
            pltpu.VMEM((3, HD, NB * ROWS), jnp.bfloat16),
            pltpu.VMEM((NB, ROWS, HD), jnp.bfloat16),
            pltpu.VMEM((2, 9 * ROWS, 2 * ROWS), jnp.float32),
            pltpu.VMEM((NB, 1, ROWS), jnp.float32),
            pltpu.VMEM((NB, 1, ROWS), jnp.float32),
            pltpu.VMEM((NB, 1, ROWS), jnp.float32),
            pltpu.VMEM((NB, HD, ROWS), jnp.float32),
            dma((3, NH)), dma((NB,)), dma((NB,)), dma((NB,)),
            dma((2, 2, NB)), dma((2, 2, NB)), dma((NB,)), dma((NH,)),
            dma((NZ,)), dma((NZ,)), dma((4,)), dma((4,)), dma((8,)), dma((8,)),
            dma((4,)), dma((4,)), dma((16,)), dma((16,)),
        ],
        compiler_params=pltpu.CompilerParams(collective_id=0, has_side_effects=True,
                                             vmem_limit_bytes=62 * 1024 * 1024),
        name="gather_and_attend",
    )(q, k, v, w)


def per_device(queries, keys, values, hidden, control, gate, out_weight):
    channels = queries.shape[-1]
    width = out_weight.shape[1]
    flat = [a.reshape(-1, channels) for a in (queries, keys, values)]
    attention, weight = gather_and_attend(*flat, out_weight)
    projected = jnp.dot(attention, weight.reshape(channels, width), preferred_element_type=jnp.float32)
    result = hidden.reshape(-1, width).astype(jnp.float32) + gate.astype(jnp.float32)[None, :] * projected
    result = result + control.reshape(-1, width).astype(jnp.float32)
    return result.astype(jnp.bfloat16).reshape(hidden.shape)


def solution(mesh):
    tokens = P(("batch", "frame"), "space", None, None, None)
    return jax.shard_map(
        per_device,
        mesh=mesh,
        in_specs=(tokens,) * 5 + (P(), P(("frame", "space"), None)),
        out_specs=tokens,
        check_vma=False,
    )
```

```python
import functools

import jax
import jax.numpy as jnp
from jax import lax
from jax.experimental import pallas as pl
from jax.experimental.pallas import tpu as pltpu
from jax.sharding import PartitionSpec as P

HD = 128
ROWS = 128
NH = 12
NB = 16
GW = 4
NY = 4
NF = 4
NZ = 8
MESH = pl.DeviceIdType.MESH
SCALE = HD ** -0.5 * 1.4426950408889634


def kernel(q_hbm, k_hbm, v_hbm, w_ref, attn, wfull,
           qbuf, kbuf, vbuf, vturn, obuf, sbuf, mbuf, abuf, lbuf, acc,
           s_snd, k_rcv, v_rcv, q_rcv, h_snd, h_rcv, o_snd, o_rcv,
           w1s, w1r, w2s, w2r, w3s, w3r, w4s, w4r, w5s, w5r):
    y, f, s = lax.axis_index("batch"), lax.axis_index("frame"), lax.axis_index("space")
    lo, z = s // NZ, s % NZ
    hi, core = f // 2, f % 2
    quarter = wfull.shape[-1] // NY
    owner = jnp.where(s < NZ, s % 4 != 3, s % 4 != 1)
    my_head = (s // 4) * 3 + s % 4 - jnp.where((s >= NZ) & (s % 4 > 1), 1, 0)
    partner = f + 1 - 2 * core
    cross = f - 1 + 2 * core
    has_cross = (f == 1) | (f == 2)
    x = hi * 2 + lo
    xr, xl = (x + 1) % 4, (x + 3) % 4
    yr, yl = (y + 1) % NY, (y + NY - 1) % NY

    def at_x(pos):
        return (y, (pos // 2) * 2 + core, (pos % 2) * NZ + z)

    def wcols(yy):
        return pl.ds(pl.multiple_of(yy * quarter, 128), quarter)

    barrier = pltpu.get_barrier_semaphore()

    def greet(i, carry):
        pl.semaphore_signal(barrier, inc=1, device_id=(y, f, (s + i) % NB), device_id_type=MESH)
        return carry

    lax.fori_loop(1, NB, greet, 0)
    other_f = (f + 2) % NF
    for dev in ((y, other_f, s), (y, other_f, (s + NZ) % NB), (yr, f, s), (yl, f, s), (y, partner, s)):
        pl.semaphore_signal(barrier, inc=1, device_id=dev, device_id_type=MESH)

    @pl.when(has_cross)
    def _():
        pl.semaphore_signal(barrier, inc=1, device_id=(y, cross, s), device_id_type=MESH)

    pl.semaphore_wait(barrier, jnp.where(has_cross, NB + 5, NB + 4))

    def remote(src, dst, snd, rcv, dev):
        return pltpu.make_async_remote_copy(
            src_ref=src, dst_ref=dst, send_sem=snd, recv_sem=rcv, device_id=dev, device_id_type=MESH)

    def await_copy(ref, sem):
        pltpu.make_async_copy(ref, ref, sem).wait()

    def w1(i):
        zz = (z + i) % NZ
        return remote(w_ref.at[:, wcols(y)], wfull.at[f, s, :, wcols(y)], w1s.at[zz], w1r.at[z],
                      (y, f, lo * NZ + zz))

    def start_w1(i, carry):
        w1(i).start()
        return carry

    pltpu.make_async_copy(w_ref.at[:, wcols(y)], wfull.at[f, s, :, wcols(y)], w1r.at[z]).start()
    lax.fori_loop(1, NZ, start_w1, 0)

    first = jnp.minimum(my_head, NH - 1)

    half = NH // 2

    def head_of(wave, i):
        top = lo if wave == 0 else 1 - lo
        h = top * half + (first + i) % half
        return h, (h // 3) * 4 + h % 3 + jnp.where((h >= half) & (h % 3 > 0), 1, 0)

    def piece(ref, h):
        return ref.at[:, pl.ds(pl.multiple_of(h * HD, HD), HD)]

    streams = ((0, k_hbm, kbuf.at[0], k_rcv), (1, v_hbm, vbuf.at[0], v_rcv), (2, q_hbm, qbuf, q_rcv))

    def send_heads(wave):
        def step(i, carry):
            h, to = head_of(wave, i)
            for row, src, dst, rcv in streams:
                @pl.when(to == s)
                def _():
                    pltpu.make_async_copy(piece(src, h), dst.at[s], rcv.at[s]).start()

                @pl.when(to != s)
                def _():
                    remote(piece(src, h), dst.at[s], s_snd.at[row, h], rcv.at[s], (y, f, to)).start()
            return carry

        lax.fori_loop(0, half, step, 0)

    send_heads(0)

    places = (x, xl, xr, (x + 2) % 4)
    layers = (y, yl, yr, (y + 2) % NY)
    halves = ((0, NZ // 2), (NZ // 2, NZ // 2))

    def block(n, m=0, side=core, part=(0, NZ)):
        pos = places[n]
        return wfull.at[(pos // 2) * 2 + side, pl.ds((pos % 2) * NZ + part[0], part[1]), :, wcols(layers[m])]

    def push(ref, snd, rcv, dev):
        return remote(ref, ref, snd, rcv, dev)

    x_own = (push(block(0), w2s.at[0], w2r.at[0], at_x(xr)), push(block(0), w2s.at[1], w2r.at[1], at_x(xl)))
    x_rel = (push(block(1, part=halves[0]), w2s.at[2], w2r.at[2], at_x(xr)),
             push(block(2, part=halves[1]), w2s.at[3], w2r.at[3], at_x(xl)))

    def y_own(d, n):
        return push(block(n), w3s.at[4 * d + n], w3r.at[4 * d + n], ((yr, yl)[d], f, s))

    def y_rel(n):
        return push(block(n, 1), w4s.at[n], w4r.at[n], (yr, f, s)) if n < 2 else \
            push(block(n, 2), w4s.at[n], w4r.at[n], (yl, f, s))

    def to_partner(m, n):
        return push(block(n, m), w5s.at[4 * m + n], w5r.at[4 * m + n], (y, partner, s))

    def spread(n):
        y_own(0, n).start()
        y_own(1, n).start()
        to_partner(0, n).start()

    def weight_z():
        lax.fori_loop(0, NZ, await_w1, 0)
        x_own[0].start()
        x_own[1].start()
        spread(0)

    def weight_x():
        await_copy(block(1), w2r.at[0])
        x_rel[0].start()
        spread(1)
        await_copy(block(2), w2r.at[1])
        x_rel[1].start()
        spread(2)

    def weight_x2():
        await_copy(block(3, part=halves[0]), w2r.at[2])
        await_copy(block(3, part=halves[1]), w2r.at[3])
        spread(3)

    def weight_y(n):
        await_copy(block(n, 1), w3r.at[n])
        if n < 2:
            y_rel(n).start()
        to_partner(1, n).start()
        await_copy(block(n, 2), w3r.at[4 + n])
        if n >= 2:
            y_rel(n).start()
        to_partner(2, n).start()

    def weight_y2(n):
        await_copy(block(n, 3), w4r.at[n])
        to_partner(3, n).start()

    def await_w1(i, carry):
        await_copy(wfull.at[f, lo * NZ + i, :, wcols(y)], w1r.at[i])
        return carry

    def forward(i):
        box = ((lo + i // NZ) % 2) * NZ + (z + NB - i) % NZ
        out = []
        for n, (buf, rcv) in enumerate(((kbuf, k_rcv), (vbuf, v_rcv))):
            out.append((buf, rcv, box,
                        remote(buf.at[0, box], buf.at[1, box], h_snd.at[n, 0, box], h_rcv.at[n, 0, box],
                               (y, partner, s)),
                        remote(buf.at[0, box], buf.at[2, box], h_snd.at[n, 1, box], h_rcv.at[n, 1, box],
                               (y, cross, s))))
        return out

    def forward_step(i, carry):
        for buf, rcv, box, near, far in forward(i):
            await_copy(buf.at[0, box], rcv.at[box])

            @pl.when(has_cross)
            def _():
                far.start()

            near.start()
        return carry

    weight_z()
    weight_x()
    send_heads(1)
    weight_steps = (weight_x2,) + tuple(functools.partial(weight_y, n) for n in range(4))

    @pl.when(owner)
    def _():
        mbuf[...] = jnp.full_like(mbuf, -1e30)
        lbuf[...] = jnp.zeros_like(lbuf)
        acc[...] = jnp.zeros_like(acc)
        weight_steps[0]()
        lax.fori_loop(0, 4, forward_step, 0)
        weight_steps[1]()
        lax.fori_loop(4, NZ, forward_step, 0)

    @pl.when(jnp.logical_not(owner))
    def _():
        for step in weight_steps:
            step()
        for n in range(4):
            weight_y2(n)

    frames = jnp.where(has_cross, 3, 2)

    def send_o(slot, box, start):
        @pl.when(s == box)
        def _():
            if start:
                pltpu.make_async_copy(obuf.at[slot], piece(attn, my_head), o_rcv.at[my_head]).start()

        @pl.when(s != box)
        def _():
            cp = remote(obuf.at[slot], piece(attn, my_head), o_snd.at[slot], o_rcv.at[my_head], (y, f, box))
            if start:
                cp.start()
            else:
                cp.wait_send()

    spans = ((0, 2), (0, 3), (0, 3), (1, 3))

    def at_row(g):
        return jnp.where(lo == 0, g, GW - 1 - g) * GW

    def score(j, r, pair, rows, slot):
        box = r * GW + 2 * pair
        q = qbuf[pl.ds(at_row(r) + 2 * pair, 2)].reshape(2 * ROWS, HD)
        tops = [[], []]
        for i, g in enumerate(rows):
            sc = lax.dot_general(kbuf[j, pl.ds(at_row(g) + pair, 3)].reshape(3 * ROWS, HD), q,
                                 (((1,), (1,)), ((), ())), preferred_element_type=jnp.float32)
            sbuf[slot, i * 3 * ROWS:(i + 1) * 3 * ROWS] = sc
            for side in (0, 1):
                k0, k1 = spans[2 * pair + side]
                tops[side].append(jnp.max(sc[k0 * ROWS:k1 * ROWS, side * ROWS:side * ROWS + ROWS],
                                          axis=0, keepdims=True))
        for side in (0, 1):
            m_old = mbuf[box + side]
            m_new = functools.reduce(jnp.maximum, tops[side], m_old)
            mbuf[box + side] = m_new
            abuf[box + side] = jnp.exp2((m_old - m_new) * SCALE)

    def blend(j, r, pair, rows, slot):
        for side in (0, 1):
            box = r * GW + 2 * pair + side
            k0, k1 = spans[2 * pair + side]
            shift = mbuf[box] * SCALE
            total = lbuf[box] * abuf[box]
            out = acc[box] * abuf[box]
            for i, g in enumerate(rows):
                sc = sbuf[slot, (3 * i + k0) * ROWS:(3 * i + k1) * ROWS, side * ROWS:side * ROWS + ROWS]
                p = jnp.exp2(sc * SCALE - shift)
                total = total + jnp.sum(p, axis=0, keepdims=True)
                c = (g * GW + pair + k0) * ROWS
                out = out + jnp.dot(vturn[j, :, c:c + (k1 - k0) * ROWS], p.astype(jnp.bfloat16),
                                    preferred_element_type=jnp.float32)
            lbuf[box] = total
            acc[box] = out

    def finish(r):
        for box in range(r * GW, r * GW + GW):
            obuf[box] = (acc[box] / lbuf[box]).T.astype(jnp.bfloat16)

    def send_row(r):
        for c in range(GW):
            send_o(r * GW + c, at_row(r) + c, True)

    def await_rows(rows):
        def at_j(j, g, c):
            b = at_row(g) + c
            await_copy(kbuf.at[j, b], h_rcv.at[0, j - 1, b])
            await_copy(vbuf.at[j, b], h_rcv.at[1, j - 1, b])

        for g in rows:
            for c in range(GW):
                at_j(1, g, c)
                await_copy(qbuf.at[at_row(g) + c], q_rcv.at[at_row(g) + c])

        @pl.when(has_cross)
        def _():
            for g in rows:
                for c in range(GW):
                    at_j(2, g, c)

    def attend(r, rows, fresh=()):
        score(0, r, 0, rows, 0)

        def one_frame(j, carry):
            for b in (g * GW + c for g in fresh for c in range(GW)):
                vturn[j, :, b * ROWS:b * ROWS + ROWS] = vbuf[j, at_row(b // GW) + b % GW].T
            score(j, r, 1, rows, 1)
            blend(j, r, 0, rows, 0)
            score(jnp.minimum(j + 1, frames - 1), r, 0, rows, 0)
            blend(j, r, 1, rows, 1)
            return carry

        lax.fori_loop(0, frames, one_frame, 0)

    @pl.when(owner)
    def _():
        await_rows((0, 1))
        attend(0, (0, 1), (0, 1))
        finish(0)
        weight_steps[2]()
        lax.fori_loop(NZ, NZ + 4, forward_step, 0)
        send_row(0)
        weight_steps[3]()
        attend(1, (0, 1))
        lax.fori_loop(NZ + 4, NB, forward_step, 0)
        weight_steps[4]()
        weight_y2(0)
        await_rows((2, 3))
        attend(1, (2,), (2,))
        finish(1)
        attend(2, (1, 2, 3), (3,))
        send_row(1)
        finish(2)
        weight_y2(1)
        weight_y2(2)
        attend(3, (2, 3))
        send_row(2)
        finish(3)
        weight_y2(3)
        send_row(3)

    def await_o(h, carry):
        await_copy(piece(attn, h), o_rcv.at[h])
        return carry

    lax.fori_loop(0, NH, await_o, 0)
    for m in range(4):
        for n in range(4):
            await_copy(block(n, m, 1 - core), w5r.at[4 * m + n])

    def drain_heads(wave):
        def step(i, carry):
            h, to = head_of(wave, i)

            @pl.when(to != s)
            def _():
                for row, src, dst, rcv in streams:
                    remote(piece(src, h), dst.at[s], s_snd.at[row, h], rcv.at[s], (y, f, to)).wait_send()
            return carry

        lax.fori_loop(0, half, step, 0)

    drain_heads(0)
    drain_heads(1)

    def drain_w1(i, carry):
        w1(i).wait_send()
        return carry

    lax.fori_loop(1, NZ, drain_w1, 0)
    for cp in x_own + x_rel:
        cp.wait_send()
    for n in range(4):
        y_own(0, n).wait_send()
        y_own(1, n).wait_send()
        y_rel(n).wait_send()
        for m in range(4):
            to_partner(m, n).wait_send()

    @pl.when(owner)
    def _():
        def drain(i, carry):
            for _, _, _, near, far in forward(i):
                near.wait_send()

                @pl.when(has_cross)
                def _():
                    far.wait_send()
            return carry

        lax.fori_loop(0, NB, drain, 0)
        for slot in range(NB):
            send_o(slot, at_row(slot // GW) + slot % GW, False)


def gather_and_attend(q, k, v, w):
    dma = pltpu.SemaphoreType.DMA
    any_spec = pl.BlockSpec(memory_space=pl.ANY)
    return pl.pallas_call(
        kernel,
        out_shape=(jax.ShapeDtypeStruct(q.shape, q.dtype),
                   jax.ShapeDtypeStruct((NF, NB) + w.shape, w.dtype)),
        in_specs=[any_spec] * 3 + [pl.BlockSpec(memory_space=pltpu.VMEM)],
        out_specs=(any_spec, any_spec),
        scratch_shapes=[
            pltpu.VMEM((NB, ROWS, HD), jnp.bfloat16),
            pltpu.VMEM((3, NB, ROWS, HD), jnp.bfloat16),
            pltpu.VMEM((3, NB, ROWS, HD), jnp.bfloat16),
            pltpu.VMEM((3, HD, NB * ROWS), jnp.bfloat16),
            pltpu.VMEM((NB, ROWS, HD), jnp.bfloat16),
            pltpu.VMEM((2, 9 * ROWS, 2 * ROWS), jnp.float32),
            pltpu.VMEM((NB, 1, ROWS), jnp.float32),
            pltpu.VMEM((NB, 1, ROWS), jnp.float32),
            pltpu.VMEM((NB, 1, ROWS), jnp.float32),
            pltpu.VMEM((NB, HD, ROWS), jnp.float32),
            dma((3, NH)), dma((NB,)), dma((NB,)), dma((NB,)),
            dma((2, 2, NB)), dma((2, 2, NB)), dma((NB,)), dma((NH,)),
            dma((NZ,)), dma((NZ,)), dma((4,)), dma((4,)), dma((8,)), dma((8,)),
            dma((4,)), dma((4,)), dma((16,)), dma((16,)),
        ],
        compiler_params=pltpu.CompilerParams(collective_id=0, has_side_effects=True,
                                             vmem_limit_bytes=62 * 1024 * 1024),
        name="gather_and_attend",
    )(q, k, v, w)


def per_device(queries, keys, values, hidden, control, gate, out_weight):
    channels = queries.shape[-1]
    width = out_weight.shape[1]
    flat = [a.reshape(-1, channels) for a in (queries, keys, values)]
    attention, weight = gather_and_attend(*flat, out_weight)
    projected = jnp.dot(attention, weight.reshape(channels, width), preferred_element_type=jnp.float32)
    result = hidden.reshape(-1, width).astype(jnp.float32) + gate.astype(jnp.float32)[None, :] * projected
    result = result + control.reshape(-1, width).astype(jnp.float32)
    return result.astype(jnp.bfloat16).reshape(hidden.shape)


def solution(mesh):
    tokens = P(("batch", "frame"), "space", None, None, None)
    return jax.shard_map(
        per_device,
        mesh=mesh,
        in_specs=(tokens,) * 5 + (P(), P(("frame", "space"), None)),
        out_specs=tokens,
        check_vma=False,
    )
```

```python
import functools

import jax
import jax.numpy as jnp
from jax import lax
from jax.experimental import pallas as pl
from jax.experimental.pallas import tpu as pltpu
from jax.sharding import PartitionSpec as P

HD = 128
ROWS = 128
NH = 12
NB = 16
GW = 4
NY = 4
NF = 4
NZ = 8
MESH = pl.DeviceIdType.MESH
SCALE = HD ** -0.5 * 1.4426950408889634


def kernel(q_hbm, k_hbm, v_hbm, w_hbm, attn, wfull,
           qbuf, kbuf, vbuf, vturn, obuf, sbuf, mbuf, abuf, lbuf, acc,
           s_snd, k_rcv, v_rcv, q_rcv, h_snd, h_rcv, o_snd, o_rcv,
           w1s, w1r, w2s, w2r, w3s, w3r, w4s, w4r, w5s, w5r):
    y, f, s = lax.axis_index("batch"), lax.axis_index("frame"), lax.axis_index("space")
    lo, z = s // NZ, s % NZ
    hi, core = f // 2, f % 2
    quarter = wfull.shape[-1] // NY
    owner = jnp.where(s < NZ, s % 4 != 3, s % 4 != 1)
    my_head = (s // 4) * 3 + s % 4 - jnp.where((s >= NZ) & (s % 4 > 1), 1, 0)
    partner = f + 1 - 2 * core
    cross = f - 1 + 2 * core
    has_cross = (f == 1) | (f == 2)
    x = hi * 2 + lo
    xr, xl = (x + 1) % 4, (x + 3) % 4
    yr, yl = (y + 1) % NY, (y + NY - 1) % NY

    def at_x(pos):
        return (y, (pos // 2) * 2 + core, (pos % 2) * NZ + z)

    def wcols(yy):
        return pl.ds(pl.multiple_of(yy * quarter, 128), quarter)

    barrier = pltpu.get_barrier_semaphore()

    def greet(i, carry):
        pl.semaphore_signal(barrier, inc=1, device_id=(y, f, (s + i) % NB), device_id_type=MESH)
        return carry

    lax.fori_loop(1, NB, greet, 0)
    other_f = (f + 2) % NF
    for dev in ((y, other_f, s), (y, other_f, (s + NZ) % NB), (yr, f, s), (yl, f, s), (y, partner, s)):
        pl.semaphore_signal(barrier, inc=1, device_id=dev, device_id_type=MESH)

    @pl.when(has_cross)
    def _():
        pl.semaphore_signal(barrier, inc=1, device_id=(y, cross, s), device_id_type=MESH)

    pl.semaphore_wait(barrier, jnp.where(has_cross, NB + 5, NB + 4))

    def remote(src, dst, snd, rcv, dev):
        return pltpu.make_async_remote_copy(
            src_ref=src, dst_ref=dst, send_sem=snd, recv_sem=rcv, device_id=dev, device_id_type=MESH)

    def await_copy(ref, sem):
        pltpu.make_async_copy(ref, ref, sem).wait()

    def w1(i):
        zz = (z + i) % NZ
        return remote(w_hbm.at[:, wcols(y)], wfull.at[f, s, :, wcols(y)], w1s.at[zz], w1r.at[z],
                      (y, f, lo * NZ + zz))

    def start_w1(i, carry):
        w1(i).start()
        return carry

    pltpu.make_async_copy(w_hbm.at[:, wcols(y)], wfull.at[f, s, :, wcols(y)], w1r.at[z]).start()
    lax.fori_loop(1, NZ, start_w1, 0)

    first = jnp.minimum(my_head, NH - 1)

    half = NH // 2

    def head_of(i):
        h = ((lo + i // half) % 2) * half + (first + i) % half
        return h, (h // 3) * 4 + h % 3 + jnp.where((h >= half) & (h % 3 > 0), 1, 0)

    def piece(ref, h):
        return ref.at[:, pl.ds(pl.multiple_of(h * HD, HD), HD)]

    streams = ((0, k_hbm, kbuf.at[0], k_rcv), (1, v_hbm, vbuf.at[0], v_rcv), (2, q_hbm, qbuf, q_rcv))

    def send_heads(which, i0=0, i1=NH):
        def step(i, carry):
            h, to = head_of(i)
            for n in which:
                row, src, dst, rcv = streams[n]

                @pl.when(to == s)
                def _():
                    pltpu.make_async_copy(piece(src, h), dst.at[s], rcv.at[s]).start()

                @pl.when(to != s)
                def _():
                    remote(piece(src, h), dst.at[s], s_snd.at[row, h], rcv.at[s], (y, f, to)).start()
            return carry

        lax.fori_loop(i0, i1, step, 0)


    places = (x, xl, xr, (x + 2) % 4)
    layers = (y, yl, yr, (y + 2) % NY)
    halves = ((0, NZ // 2), (NZ // 2, NZ // 2))

    def block(n, m=0, side=core, part=(0, NZ)):
        pos = places[n]
        return wfull.at[(pos // 2) * 2 + side, pl.ds((pos % 2) * NZ + part[0], part[1]), :, wcols(layers[m])]

    def push(ref, snd, rcv, dev):
        return remote(ref, ref, snd, rcv, dev)

    x_own = (push(block(0), w2s.at[0], w2r.at[0], at_x(xr)), push(block(0), w2s.at[1], w2r.at[1], at_x(xl)))
    x_rel = (push(block(1, part=halves[0]), w2s.at[2], w2r.at[2], at_x(xr)),
             push(block(2, part=halves[1]), w2s.at[3], w2r.at[3], at_x(xl)))

    def y_own(d, n):
        return push(block(n), w3s.at[4 * d + n], w3r.at[4 * d + n], ((yr, yl)[d], f, s))

    def y_rel(n):
        return push(block(n, 1), w4s.at[n], w4r.at[n], (yr, f, s)) if n < 2 else \
            push(block(n, 2), w4s.at[n], w4r.at[n], (yl, f, s))

    def to_partner(m, n):
        return push(block(n, m), w5s.at[4 * m + n], w5r.at[4 * m + n], (y, partner, s))

    def spread(n):
        y_own(0, n).start()
        y_own(1, n).start()
        to_partner(0, n).start()

    def weight_z():
        lax.fori_loop(0, NZ, await_w1, 0)
        x_own[0].start()
        x_own[1].start()
        spread(0)

    def weight_x():
        await_copy(block(1), w2r.at[0])
        x_rel[0].start()
        spread(1)
        await_copy(block(2), w2r.at[1])
        x_rel[1].start()
        spread(2)

    def weight_x2():
        await_copy(block(3, part=halves[0]), w2r.at[2])
        await_copy(block(3, part=halves[1]), w2r.at[3])
        spread(3)

    def weight_y(n):
        await_copy(block(n, 1), w3r.at[n])
        if n < 2:
            y_rel(n).start()
        to_partner(1, n).start()
        await_copy(block(n, 2), w3r.at[4 + n])
        if n >= 2:
            y_rel(n).start()
        to_partner(2, n).start()

    def weight_y2(n):
        await_copy(block(n, 3), w4r.at[n])
        to_partner(3, n).start()

    def await_w1(i, carry):
        await_copy(wfull.at[f, lo * NZ + i, :, wcols(y)], w1r.at[i])
        return carry

    def forward(i):
        box = ((lo + i // NZ) % 2) * NZ + (z + NB - i) % NZ
        out = []
        for n, (buf, rcv) in enumerate(((kbuf, k_rcv), (vbuf, v_rcv))):
            out.append((buf, rcv, box,
                        remote(buf.at[0, box], buf.at[1, box], h_snd.at[n, 0, box], h_rcv.at[n, 0, box],
                               (y, partner, s)),
                        remote(buf.at[0, box], buf.at[2, box], h_snd.at[n, 1, box], h_rcv.at[n, 1, box],
                               (y, cross, s))))
        return out

    def forward_step(i, carry):
        for buf, rcv, box, near, far in forward(i):
            await_copy(buf.at[0, box], rcv.at[box])

            @pl.when(has_cross)
            def _():
                far.start()

            near.start()
        return carry

    weight_z()
    send_heads((0, 1))
    send_heads((2,))
    weight_steps = (weight_x, weight_x2) + tuple(functools.partial(weight_y, n) for n in range(4))

    @pl.when(owner)
    def _():
        mbuf[...] = jnp.full_like(mbuf, -1e30)
        lbuf[...] = jnp.zeros_like(lbuf)
        acc[...] = jnp.zeros_like(acc)
        marks = (0, 0, 4, 8, 12, 14, NB)
        for step, i0, i1 in zip(weight_steps, marks, marks[1:]):
            step()
            lax.fori_loop(i0, i1, forward_step, 0)

    @pl.when(jnp.logical_not(owner))
    def _():
        for step in weight_steps:
            step()
        for n in range(4):
            weight_y2(n)

    frames = jnp.where(has_cross, 3, 2)

    def send_o(box, start):
        @pl.when(s == box)
        def _():
            if start:
                pltpu.make_async_copy(obuf.at[box], piece(attn, my_head), o_rcv.at[my_head]).start()

        @pl.when(s != box)
        def _():
            cp = remote(obuf.at[box], piece(attn, my_head), o_snd.at[box], o_rcv.at[my_head], (y, f, box))
            if start:
                cp.start()
            else:
                cp.wait_send()

    spans = ((0, 2), (0, 3), (0, 3), (1, 3))

    def around(k):
        r = k // 2
        return r, k % 2, range(max(r - 1, 0), min(r + 2, GW))

    def score(j, k):
        r, pair, rows = around(k)
        box = r * GW + 2 * pair
        q = qbuf[box:box + 2].reshape(2 * ROWS, HD)
        tops = [[], []]
        for i, g in enumerate(rows):
            sc = lax.dot_general(kbuf[j, g * GW + pair:g * GW + pair + 3].reshape(3 * ROWS, HD), q,
                                 (((1,), (1,)), ((), ())), preferred_element_type=jnp.float32)
            sbuf[k % 2, i * 3 * ROWS:(i + 1) * 3 * ROWS] = sc
            for side in (0, 1):
                k0, k1 = spans[2 * pair + side]
                tops[side].append(jnp.max(sc[k0 * ROWS:k1 * ROWS, side * ROWS:side * ROWS + ROWS],
                                          axis=0, keepdims=True))
        for side in (0, 1):
            m_old = mbuf[box + side]
            m_new = functools.reduce(jnp.maximum, tops[side], m_old)
            mbuf[box + side] = m_new
            abuf[box + side] = jnp.exp2((m_old - m_new) * SCALE)

    def blend(j, k):
        r, pair, rows = around(k)
        for side in (0, 1):
            box = r * GW + 2 * pair + side
            k0, k1 = spans[2 * pair + side]
            shift = mbuf[box] * SCALE
            total = lbuf[box] * abuf[box]
            out = acc[box] * abuf[box]
            for i, g in enumerate(rows):
                sc = sbuf[k % 2, (3 * i + k0) * ROWS:(3 * i + k1) * ROWS, side * ROWS:side * ROWS + ROWS]
                p = jnp.exp2(sc * SCALE - shift)
                total = total + jnp.sum(p, axis=0, keepdims=True)
                c = (g * GW + pair + k0) * ROWS
                out = out + jnp.dot(vturn[j, :, c:c + (k1 - k0) * ROWS], p.astype(jnp.bfloat16),
                                    preferred_element_type=jnp.float32)
            lbuf[box] = total
            acc[box] = out

    def finish(r):
        for box in range(r * GW, r * GW + GW):
            obuf[box] = (acc[box] / lbuf[box]).T.astype(jnp.bfloat16)

    def send_row(r):
        for box in range(r * GW, r * GW + GW):
            send_o(box, True)

    def attend_row(r):
        fresh = [g * GW + c for g in (range(0, 2) if r == 0 else range(r + 1, min(r + 2, GW))) for c in range(GW)]

        def await_halo(j):
            for b in fresh:
                await_copy(kbuf.at[j, b], h_rcv.at[0, j - 1, b])
                await_copy(vbuf.at[j, b], h_rcv.at[1, j - 1, b])

        await_halo(1)

        @pl.when(has_cross)
        def _():
            await_halo(2)

        for box in range(r * GW, r * GW + GW):
            await_copy(qbuf.at[box], q_rcv.at[box])
        score(0, 2 * r)
        if r:
            send_row(r - 1)

        def one_frame(j, carry):
            for b in fresh:
                vturn[j, :, b * ROWS:b * ROWS + ROWS] = vbuf[j, b].T
            score(j, 2 * r + 1)
            blend(j, 2 * r)
            score(jnp.minimum(j + 1, frames - 1), 2 * r)
            blend(j, 2 * r + 1)
            return carry

        lax.fori_loop(0, frames, one_frame, 0)
        finish(r)

    @pl.when(owner)
    def _():
        for r in range(GW):
            attend_row(r)
            if r >= 2:
                weight_y2(2 * r - 4)
                weight_y2(2 * r - 3)
        send_row(GW - 1)

    def await_o(h, carry):
        await_copy(piece(attn, h), o_rcv.at[h])
        return carry

    lax.fori_loop(0, NH, await_o, 0)
    for m in range(4):
        for n in range(4):
            await_copy(block(n, m, 1 - core), w5r.at[4 * m + n])

    def drain_heads(i, carry):
        h, to = head_of(i)

        @pl.when(to != s)
        def _():
            for row, src, dst, rcv in streams:
                remote(piece(src, h), dst.at[s], s_snd.at[row, h], rcv.at[s], (y, f, to)).wait_send()
        return carry

    lax.fori_loop(0, NH, drain_heads, 0)

    def drain_w1(i, carry):
        w1(i).wait_send()
        return carry

    lax.fori_loop(1, NZ, drain_w1, 0)
    for cp in x_own + x_rel:
        cp.wait_send()
    for n in range(4):
        y_own(0, n).wait_send()
        y_own(1, n).wait_send()
        y_rel(n).wait_send()
        for m in range(4):
            to_partner(m, n).wait_send()

    @pl.when(owner)
    def _():
        def drain(i, carry):
            for _, _, _, near, far in forward(i):
                near.wait_send()

                @pl.when(has_cross)
                def _():
                    far.wait_send()
            return carry

        lax.fori_loop(0, NB, drain, 0)
        for box in range(NB):
            send_o(box, False)


def gather_and_attend(q, k, v, w):
    dma = pltpu.SemaphoreType.DMA
    any_spec = pl.BlockSpec(memory_space=pl.ANY)
    return pl.pallas_call(
        kernel,
        out_shape=(jax.ShapeDtypeStruct(q.shape, q.dtype),
                   jax.ShapeDtypeStruct((NF, NB) + w.shape, w.dtype)),
        in_specs=[any_spec] * 4,
        out_specs=(any_spec, any_spec),
        scratch_shapes=[
            pltpu.VMEM((NB, ROWS, HD), jnp.bfloat16),
            pltpu.VMEM((3, NB, ROWS, HD), jnp.bfloat16),
            pltpu.VMEM((3, NB, ROWS, HD), jnp.bfloat16),
            pltpu.VMEM((3, HD, NB * ROWS), jnp.bfloat16),
            pltpu.VMEM((NB, ROWS, HD), jnp.bfloat16),
            pltpu.VMEM((2, 9 * ROWS, 2 * ROWS), jnp.float32),
            pltpu.VMEM((NB, 1, ROWS), jnp.float32),
            pltpu.VMEM((NB, 1, ROWS), jnp.float32),
            pltpu.VMEM((NB, 1, ROWS), jnp.float32),
            pltpu.VMEM((NB, HD, ROWS), jnp.float32),
            dma((3, NH)), dma((NB,)), dma((NB,)), dma((NB,)),
            dma((2, 2, NB)), dma((2, 2, NB)), dma((NB,)), dma((NH,)),
            dma((NZ,)), dma((NZ,)), dma((4,)), dma((4,)), dma((8,)), dma((8,)),
            dma((4,)), dma((4,)), dma((16,)), dma((16,)),
        ],
        compiler_params=pltpu.CompilerParams(collective_id=0, has_side_effects=True,
                                             vmem_limit_bytes=62 * 1024 * 1024),
        name="gather_and_attend",
    )(q, k, v, w)


def per_device(queries, keys, values, hidden, control, gate, out_weight):
    channels = queries.shape[-1]
    width = out_weight.shape[1]
    flat = [a.reshape(-1, channels) for a in (queries, keys, values)]
    attention, weight = gather_and_attend(*flat, out_weight)
    projected = jnp.dot(attention, weight.reshape(channels, width), preferred_element_type=jnp.float32)
    result = hidden.reshape(-1, width).astype(jnp.float32) + gate.astype(jnp.float32)[None, :] * projected
    result = result + control.reshape(-1, width).astype(jnp.float32)
    return result.astype(jnp.bfloat16).reshape(hidden.shape)


def solution(mesh):
    tokens = P(("batch", "frame"), "space", None, None, None)
    return jax.shard_map(
        per_device,
        mesh=mesh,
        in_specs=(tokens,) * 5 + (P(), P(("frame", "space"), None)),
        out_specs=tokens,
        check_vma=False,
    )
```
